32 devices in a mesh: section: 2 (over core), dom: 16 (over z, y, x).
Axes of the slice: x: 2, y: 2, z: 4, core: 2. Of those that a mesh axis runs over, the one named last changes fastest.
Arguments:
- blocks: float32 [16, 32, 6, 128, 128], P('section', 'dom'), may hold values from -0.21875 to 0.21875
- column_index: int32 [16, 32, 6], P('section', 'dom'), may hold values from 0 to 31
- block_period: int32 [16, 32, 6], P('section', 'dom'), may hold values from 0 to 15, as said below
- cost_vector: float32 [16, 4096], P('section', 'dom'), may hold values from -6 to 6
- demand: float32 [16, 4096], P('section', 'dom'), may hold values from -12 to 12
- primal_start: float32 [16, 4096], P('section', 'dom'), may hold values from 0 to 2
- dual_start: float32 [16, 4096], P('section', 'dom'), may hold values from -3 to 3
- primal_weight: float32 [1], replicated, may hold values from 0.5 to 2
Outputs:
- primal_final: float32 [16, 4096], P('section', 'dom')
- dual_final: float32 [16, 4096], P('section', 'dom')
The draws below stay inside these ranges and needn't reach their ends.
Inputs may be any that keep to these rules, and one draw needn't show every extreme that they name: block_period[p, r, k] is p or p - 1; it is p for k = 0 and for p = 0.
All inputs are finite; a program needn't handle non-finite values.
Results may differ from the reference program's by a relative error of at most 0.00011.
Values sent between devices are 32-bit elements; how exact they have to be, the bound alone decides.
A program may use at most 64 MiB of HBM per device.

```python
import math
import jax
import jax.numpy as jnp
from jax import lax

B = 128
NNZB = 6
PERIODS = 16
NBP = 32


def draw_block_period(key, part):
    own_period = jnp.arange(PERIODS, dtype=jnp.int32)[:, None, None]
    stepped = jax.random.randint(key, (PERIODS, NBP, NNZB), 0, 2).astype(jnp.int32)
    later_slot = (jnp.arange(NNZB, dtype=jnp.int32) > 0).astype(jnp.int32)[None, None, :]
    later_period = (own_period > 0).astype(jnp.int32)
    return (own_period - stepped * later_slot * later_period).astype(jnp.int32)


def draw_demand(key, part):
    rising = 1.0 + 2.0 * jnp.arange(PERIODS, dtype=jnp.float32)[:, None] / max(PERIODS - 1, 1)
    base_values = jax.random.truncated_normal(key, -4.0, 4.0, (PERIODS, NBP * B), jnp.float32)
    values = base_values * rising
    return values.astype(jnp.float32)


def with_ends(result, own_key, low, largest):
    extent = result.shape
    place = [jax.random.randint(jax.random.fold_in(own_key, axis), (), 0, extent[axis]) for axis in range(len(extent))]
    result = result.at[tuple(place)].set(low)
    longest = extent.index(max(extent))
    place[longest] = (place[longest] + 1) % extent[longest]
    return result.at[tuple(place)].set(largest)


def levels(rng, shape, pieces, smallest, largest):
    gain, own = 1.0, jax.random.fold_in(rng, 6)
    for dim, blocks in pieces:
        heights = jnp.exp(jax.random.uniform(jax.random.fold_in(own, dim), (blocks,), jnp.float32, smallest / len(pieces), largest / len(pieces)))
        gain = gain * jnp.repeat(heights, shape[dim] // blocks).reshape([-1 if axis == dim else 1 for axis in range(len(shape))])
    return gain


def scatter_about(stream_key, dims, width, limit, cuts=(), kind=jnp.bfloat16):
    result = jax.random.normal(stream_key, dims, jnp.float32) * width
    if len(cuts) > 0:
        result = levels(stream_key, dims, cuts, -0.22, 0.18) * result
    return jnp.clip(result, min=-limit, max=limit).astype(kind)


def setup_inputs(seed: int = 0) -> dict:
    seeds = jax.random.split(jax.random.key(seed), 9)
    return {
        "blocks": scatter_about(seeds[0], (PERIODS, NBP, NNZB, B, B), (NNZB * B) ** -0.5, 0.21875, ((0, 2), (1, 16)), jnp.float32),
        "column_index": with_ends(jax.random.randint(seeds[1], (PERIODS, NBP, NNZB), 0, NBP), jax.random.fold_in(seeds[1], 1), 0, NBP - 1).astype(jnp.int32),
        "block_period": draw_block_period(jax.random.fold_in(seeds[8], 71), 0),
        "cost_vector": scatter_about(seeds[3], (PERIODS, NBP * B), 1.0, 6.0, ((0, 2), (1, 16)), jnp.float32),
        "demand": draw_demand(jax.random.fold_in(seeds[8], 71), 0),
        "primal_start": jnp.clip(2.0 * jax.random.uniform(seeds[5], (PERIODS, NBP * B), jnp.float32) ** levels(seeds[5], (PERIODS, NBP * B), ((0, 2), (1, 16)), -0.2, 0.2), 0.0, 2.0),
        "dual_start": scatter_about(seeds[6], (PERIODS, NBP * B), 0.5, 3.0, ((0, 2), (1, 16)), jnp.float32),
        "primal_weight": jnp.clip(jnp.exp(jax.random.uniform(seeds[7], (1,), jnp.float32, math.log(0.5), math.log(2.0))), 0.5, 2.0),
    }


step_scale = 0.4
epsilon = 1e-06

def forward(blocks, column_index, block_period, field):
    field_blocks = field.reshape(PERIODS, NBP, B)
    picked = field_blocks[block_period, column_index]
    product = jnp.einsum('prkij,prkj->pri', blocks, picked, precision=lax.Precision.HIGHEST)
    return product.reshape(PERIODS, NBP * B)

def adjoint(blocks, column_index, block_period, field):
    field_blocks = field.reshape(PERIODS, NBP, B)
    block_terms = jnp.einsum('prkij,pri->prkj', blocks, field_blocks, precision=lax.Precision.HIGHEST)
    segment_ids = (block_period * NBP + column_index).reshape(-1).astype(jnp.int32)
    summed = jax.ops.segment_sum(block_terms.reshape(-1, B), segment_ids, num_segments=PERIODS * NBP)
    return summed.reshape(PERIODS, NBP * B)

def reference(blocks, column_index, block_period, cost_vector, demand, primal_start, dual_start, primal_weight):
    weight_now = primal_weight[0]
    tau_first = step_scale / weight_now
    sigma_first = step_scale * weight_now
    primal_one = jnp.maximum(0.0, primal_start - tau_first * (cost_vector - adjoint(blocks, column_index, block_period, dual_start)))
    dual_one = dual_start + sigma_first * (demand - forward(blocks, column_index, block_period, 2.0 * primal_one - primal_start))
    move_primal = jnp.sum((primal_one - primal_start) ** 2)
    move_dual = jnp.sum((dual_one - dual_start) ** 2)
    weight_next = jnp.sqrt(weight_now * jnp.sqrt((move_dual + epsilon) / (move_primal + epsilon)))
    tau_second = step_scale / weight_next
    sigma_second = step_scale * weight_next
    primal_final = jnp.maximum(0.0, primal_one - tau_second * (cost_vector - adjoint(blocks, column_index, block_period, dual_one)))
    dual_final = dual_one + sigma_second * (demand - forward(blocks, column_index, block_period, 2.0 * primal_final - primal_one))
    return (primal_final, dual_final)
```

```python
import functools

import jax
import jax.numpy as jnp
from jax import lax
from jax.experimental import pallas as pl
from jax.experimental.pallas import tpu as pltpu
from jax.sharding import PartitionSpec as P

step_scale = 0.4
epsilon = 1e-06
MESH = pl.DeviceIdType.MESH
BF = jnp.bfloat16
F32 = jnp.float32


def kernel_body(
    S, D, NP, NB, K, B,
    blocks, ci, bp, cost, demand, x0r, y0r, pw,
    xo, yo,
    bv, onehot, terms, wrow, ps, pb, ra, rb, xs, xb, g, gb, x1s, y1s, ds, dg, es, eg,
    bsem, snd, rcv_a, rcv_f, snd_d, rcv_d, snd_e, rcv_e,
):
    R = NB * NP
    TP = terms.shape[1]
    N = S * D
    me_s = lax.axis_index("section")
    me_d = lax.axis_index("dom")
    me = me_s * D + me_d
    prev_s = lax.rem(me_s + S - 1, S)
    next_s = lax.rem(me_s + 1, S)

    barrier = pltpu.get_barrier_semaphore()

    def greet(t, _):
        other = lax.rem(me + t, N)
        pl.semaphore_signal(
            barrier,
            inc=1,
            device_id={"section": lax.div(other, D), "dom": lax.rem(other, D)},
            device_id_type=MESH,
        )
        return 0

    for p in range(NP):
        pltpu.make_async_copy(blocks.at[p], bv.at[p], bsem.at[p]).start()
    lax.fori_loop(1, N, greet, 0)

    def own_rows(ref):
        return jnp.concatenate([ref[:, c * B : (c + 1) * B] for c in range(NB)], axis=0)

    lane = lax.broadcasted_iota(jnp.int32, (1, NP * TP), 1)
    target = jnp.full((1, NP * TP), -1, jnp.int32)
    for p in range(NP):
        for r in range(NB):
            for k in range(K):
                q = bp[p, r, k] - me_s * NP
                col = ci[p, r, k]
                d = lax.div(col, NB)
                c = col - d * NB
                row = jnp.where(q < 0, D * R + col, d * R + c * NP + q)
                target = jnp.where(lane == p * TP + r * K + k, row, target)
    M = onehot.shape[0]
    rows_m = lax.broadcasted_iota(jnp.int32, (M, NP * TP), 0)
    onehot[...] = jnp.where(rows_m == target, 1.0, 0.0).astype(BF)
    terms[...] = jnp.zeros_like(terms)

    ii = lax.broadcasted_iota(jnp.int32, (B, B), 0)
    jj = lax.broadcasted_iota(jnp.int32, (B, B), 1)
    eye = ii == jj
    riota = lax.broadcasted_iota(jnp.int32, (R, B), 0)

    def main_copy(src, dst, recv, o):
        d = lax.rem(me_d + o, D)
        return pltpu.make_async_remote_copy(
            src_ref=src(d), dst_ref=dst, send_sem=snd.at[0, o], recv_sem=recv.at[0, o],
            device_id={"section": me_s, "dom": d}, device_id_type=MESH,
        )

    def edge_copy(src, dst, recv, sec, o):
        d = lax.rem(me_d + o, D)
        return pltpu.make_async_remote_copy(
            src_ref=src(d), dst_ref=dst, send_sem=snd.at[1, o], recv_sem=recv.at[1, o],
            device_id={"section": sec, "dom": d}, device_id_type=MESH,
        )

    def loop(lo, hi, f):
        def step(o, _):
            f(o)
            return 0

        lax.fori_loop(lo, hi, step, 0)

    def my_rows(ref_at, d):
        return ref_at[pl.ds(pl.multiple_of(d * R, R), R)]

    def adjoint_terms(w, first):
        wrow[...] = w

        def period(p, _):
            if first:
                pltpu.make_async_copy(blocks.at[p], bv.at[p], bsem.at[p]).wait()
            for r in range(NB):
                wv = wrow[pl.ds(r * NP + p, 1), :]
                col = jnp.sum(
                    jnp.where(eye, jnp.broadcast_to(wv, (B, B)), 0.0), axis=1, keepdims=True
                )
                wb = jnp.broadcast_to(col, (B, B))
                for k in range(K):
                    terms[p, r * K + k : r * K + k + 1, :] = jnp.sum(
                        bv[p, r, k] * wb, axis=0, keepdims=True
                    )
            return 0

        lax.fori_loop(0, NP, period, 0)
        t = terms[...].reshape(NP * TP, B)
        hi = t.astype(BF)
        rest = t - hi.astype(F32)
        mid = rest.astype(BF)
        low = (rest - mid.astype(F32)).astype(BF)
        oh = onehot[...]
        part = (
            jnp.dot(oh, low, preferred_element_type=F32)
            + jnp.dot(oh, mid, preferred_element_type=F32)
        ) + jnp.dot(oh, hi, preferred_element_type=F32)
        ps[...] = part[: D * R]
        for d in range(D):
            pb[d] = part[D * R + d * NB : D * R + (d + 1) * NB]

    def adjoint_sends(i):
        src = lambda d: my_rows(ps.at, d)
        main = lambda o: main_copy(src, my_rows(ra.at[i].at, me_d), rcv_a.at[i], o)
        edge = lambda o: edge_copy(lambda d: pb.at[d], rb.at[i, me_d], rcv_a.at[i], prev_s, o)
        loop(1, D, lambda o: main(o).start())
        loop(0, D, lambda o: edge(o).start())
        return main, edge

    def adjoint_result(i, main, edge):
        ra[i, pl.ds(pl.multiple_of(me_d * R, R), R), :] = ps[
            pl.ds(pl.multiple_of(me_d * R, R), R), :
        ]
        loop(1, D, lambda o: main(o).wait())
        loop(0, D, lambda o: edge(o).wait())
        total = ra[i, 0:R, :]
        rim = rb[i, 0]
        for d in range(1, D):
            total = total + ra[i, d * R : (d + 1) * R, :]
            rim = rim + rb[i, d]
        for c in range(NB):
            total = total + jnp.where(
                riota == c * NP + NP - 1, jnp.broadcast_to(rim[c : c + 1], (R, B)), 0.0
            )
        return total

    def forward(i, xbar):
        xs[...] = xbar
        for c in range(NB):
            xb[c : c + 1, :] = xbar[c * NP + NP - 1 : c * NP + NP]
        main = lambda o: main_copy(lambda d: xs, my_rows(g.at[i].at, me_d), rcv_f.at[i], o)
        edge = lambda o: edge_copy(lambda d: xb, gb.at[i, me_d], rcv_f.at[i], next_s, o)
        loop(1, D, lambda o: main(o).start())
        loop(0, D, lambda o: edge(o).start())
        g[i, pl.ds(pl.multiple_of(me_d * R, R), R), :] = xbar
        loop(1, D, lambda o: main(o).wait())
        loop(0, D, lambda o: edge(o).wait())

        def period(p, y):
            for r in range(NB):
                acc = None
                for k in range(K):
                    q = bp[p, r, k] - me_s * NP
                    col = ci[p, r, k]
                    d = lax.div(col, NB)
                    c = col - d * NB
                    row = d * R + c * NP + jnp.maximum(q, 0)
                    xv = g[i, pl.ds(row, 1), :]
                    if k > 0:
                        xv = jnp.where(q < 0, gb[i, d, pl.ds(c, 1), :], xv)
                    term = bv[p, r, k] * jnp.broadcast_to(xv, (B, B))
                    acc = term if acc is None else acc + term
                y = jnp.where(jj == r * NP + p, jnp.sum(acc, axis=1, keepdims=True), y)
            return y

        y = lax.fori_loop(0, NP, period, jnp.zeros((B, B), F32))
        return y.T[:R]

    w0 = jnp.full((1, B), pw[0], F32)
    tau0 = step_scale / w0
    sigma0 = step_scale * w0

    adjoint_terms(own_rows(y0r), True)
    pl.semaphore_wait(barrier, N - 1)
    main, edge = adjoint_sends(0)
    at = adjoint_result(0, main, edge)
    x0 = own_rows(x0r)
    x1 = jnp.maximum(0.0, x0 - tau0 * (own_rows(cost) - at))
    x1s[...] = x1
    ax = forward(0, 2.0 * x1 - x0)
    y0 = own_rows(y0r)
    y1 = y0 + sigma0 * (own_rows(demand) - ax)
    y1s[...] = y1
    ds[0:1, :] = jnp.sum((x1s[...] - own_rows(x0r)) ** 2, axis=0, keepdims=True)
    ds[1:2, :] = jnp.sum((y1 - y0) ** 2, axis=0, keepdims=True)

    def dom_sum(o):
        d = lax.rem(me_d + o, D)
        return pltpu.make_async_remote_copy(
            src_ref=ds, dst_ref=dg.at[me_d], send_sem=snd_d.at[o], recv_sem=rcv_d.at[o],
            device_id={"section": me_s, "dom": d}, device_id_type=MESH,
        )

    def section_sum(o):
        s = lax.rem(me_s + o, S)
        return pltpu.make_async_remote_copy(
            src_ref=es, dst_ref=eg.at[me_s], send_sem=snd_e.at[o], recv_sem=rcv_e.at[o],
            device_id={"section": s, "dom": me_d}, device_id_type=MESH,
        )

    loop(1, D, lambda o: dom_sum(o).start())
    dg[me_d] = ds[...]
    adjoint_terms(y1, False)
    main, edge = adjoint_sends(1)
    loop(1, D, lambda o: dom_sum(o).wait())
    moved = dg[0]
    for d in range(1, D):
        moved = moved + dg[d]
    es[...] = moved
    loop(1, S, lambda o: section_sum(o).start())
    eg[me_s] = moved
    loop(1, S, lambda o: section_sum(o).wait())
    moved = eg[0]
    for s in range(1, S):
        moved = moved + eg[s]
    moved = jnp.sum(moved, axis=1, keepdims=True)
    dx = jnp.broadcast_to(moved[0:1], (1, B))
    dy = jnp.broadcast_to(moved[1:2], (1, B))
    omega = jnp.sqrt(w0 * jnp.sqrt((dy + epsilon) / (dx + epsilon)))
    tau1 = step_scale / omega
    sigma1 = step_scale * omega
    at = adjoint_result(1, main, edge)
    x1 = x1s[...]
    x2 = jnp.maximum(0.0, x1 - tau1 * (own_rows(cost) - at))
    for c in range(NB):
        xo[:, c * B : (c + 1) * B] = x2[c * NP : (c + 1) * NP]
    ax = forward(1, 2.0 * x2 - x1)
    y2 = y1s[...] + sigma1 * (own_rows(demand) - ax)
    for c in range(NB):
        yo[:, c * B : (c + 1) * B] = y2[c * NP : (c + 1) * NP]


def on_device(S, D, blocks, ci, bp, cost, demand, x0, y0, pw):
    NP, NB, K, B, _ = blocks.shape
    R = NB * NP
    TP = -(-NB * K // 8) * 8
    M = D * R + D * NB
    vmem = pl.BlockSpec(memory_space=pltpu.VMEM)
    smem = pl.BlockSpec(memory_space=pltpu.SMEM)
    hbm = pl.BlockSpec(memory_space=pl.ANY)
    V = lambda *s: pltpu.VMEM(s, F32)
    sem = lambda *s: pltpu.SemaphoreType.DMA(s)
    return pl.pallas_call(
        functools.partial(kernel_body, S, D, NP, NB, K, B),
        out_shape=(
            jax.ShapeDtypeStruct(x0.shape, F32),
            jax.ShapeDtypeStruct(y0.shape, F32),
        ),
        in_specs=[hbm, smem, smem, vmem, vmem, vmem, vmem, smem],
        out_specs=(vmem, vmem),
        scratch_shapes=[
            V(NP, NB, K, B, B),
            pltpu.VMEM((M, NP * TP), BF),
            V(NP, TP, B),
            V(R, B),
            V(D * R, B),
            V(D, NB, B),
            V(2, D * R, B),
            V(2, D, NB, B),
            V(R, B),
            V(NB, B),
            V(2, D * R, B),
            V(2, D, NB, B),
            V(R, B),
            V(R, B),
            V(2, B),
            V(D, 2, B),
            V(2, B),
            V(S, 2, B),
            sem(NP),
            sem(2, D),
            sem(2, 2, D),
            sem(2, 2, D),
            sem(D),
            sem(D),
            sem(S),
            sem(S),
        ],
        compiler_params=pltpu.CompilerParams(
            collective_id=0, has_side_effects=True, vmem_limit_bytes=48 * 1024 * 1024
        ),
    )(blocks, ci, bp, cost, demand, x0, y0, pw)


def solution(mesh):
    return jax.shard_map(
        functools.partial(on_device, mesh.shape["section"], mesh.shape["dom"]),
        mesh=mesh,
        in_specs=(
            P("section", "dom", None, None, None),
            P("section", "dom", None),
            P("section", "dom", None),
            P("section", "dom"),
            P("section", "dom"),
            P("section", "dom"),
            P("section", "dom"),
            P(),
        ),
        out_specs=(P("section", "dom"), P("section", "dom")),
        check_vma=False,
    )
```

```python
import functools

import jax
import jax.numpy as jnp
from jax import lax
from jax.experimental import pallas as pl
from jax.experimental.pallas import tpu as pltpu
from jax.sharding import PartitionSpec as P

step_scale = 0.4
epsilon = 1e-06
MESH = pl.DeviceIdType.MESH
BF = jnp.bfloat16
F32 = jnp.float32


def kernel_body(
    S, D, NP, NB, K, B,
    blocks, ci_in, bp_in, cost_in, demand_in, x0_in, y0_in, pw,
    xo, yo,
    ci, bp, cost, demand, x0r, y0r, isem,
    bv, onehot, terms, wrow, ps, pb, ra, rb, xs, xb, g, gb, x1s, y1s, ds, dg, es, eg,
    bsem, snd, rcv_a, rcv_f, snd_d, rcv_d, snd_e, rcv_e,
):
    R = NB * NP
    TP = terms.shape[1]
    N = S * D
    me_s = lax.axis_index("section")
    me_d = lax.axis_index("dom")
    me = me_s * D + me_d
    prev_s = lax.rem(me_s + S - 1, S)
    next_s = lax.rem(me_s + 1, S)

    barrier = pltpu.get_barrier_semaphore()

    def greet(t, _):
        other = lax.rem(me + t, N)
        pl.semaphore_signal(
            barrier,
            inc=1,
            device_id={"section": lax.div(other, D), "dom": lax.rem(other, D)},
            device_id_type=MESH,
        )
        return 0

    staged = [
        pltpu.make_async_copy(a, b, isem.at[i])
        for i, (a, b) in enumerate(
            ((y0_in, y0r), (ci_in, ci), (bp_in, bp), (cost_in, cost), (x0_in, x0r), (demand_in, demand))
        )
    ]
    for c in staged[:3]:
        c.start()
    for p in range(NP):
        pltpu.make_async_copy(blocks.at[p], bv.at[p], bsem.at[p]).start()
    for c in staged[3:]:
        c.start()
    lax.fori_loop(1, N, greet, 0)

    for c in staged[:3]:
        c.wait()

    def own_rows(ref):
        return jnp.concatenate([ref[:, c * B : (c + 1) * B] for c in range(NB)], axis=0)

    lane = lax.broadcasted_iota(jnp.int32, (1, NP * TP), 1)
    target = jnp.full((1, NP * TP), -1, jnp.int32)
    for p in range(NP):
        for r in range(NB):
            for k in range(K):
                q = bp[k, r, p] - me_s * NP
                col = ci[k, r, p]
                d = lax.div(col, NB)
                c = col - d * NB
                row = jnp.where(q < 0, D * R + col, d * R + c * NP + q)
                target = jnp.where(lane == p * TP + r * K + k, row, target)
    M = onehot.shape[0]
    rows_m = lax.broadcasted_iota(jnp.int32, (M, NP * TP), 0)
    onehot[...] = jnp.where(rows_m == target, 1.0, 0.0).astype(BF)
    terms[...] = jnp.zeros_like(terms)

    ii = lax.broadcasted_iota(jnp.int32, (B, B), 0)
    jj = lax.broadcasted_iota(jnp.int32, (B, B), 1)
    eye = ii == jj
    riota = lax.broadcasted_iota(jnp.int32, (R, B), 0)

    def main_copy(src, dst, recv, o):
        d = lax.rem(me_d + o, D)
        return pltpu.make_async_remote_copy(
            src_ref=src(d), dst_ref=dst, send_sem=snd.at[0, o], recv_sem=recv.at[0, o],
            device_id={"section": me_s, "dom": d}, device_id_type=MESH,
        )

    def edge_copy(src, dst, recv, sec, o):
        d = lax.rem(me_d + o, D)
        return pltpu.make_async_remote_copy(
            src_ref=src(d), dst_ref=dst, send_sem=snd.at[1, o], recv_sem=recv.at[1, o],
            device_id={"section": sec, "dom": d}, device_id_type=MESH,
        )

    def loop(lo, hi, f):
        def step(o, _):
            f(o)
            return 0

        lax.fori_loop(lo, hi, step, 0)

    def my_rows(ref_at, d):
        return ref_at[pl.ds(pl.multiple_of(d * R, R), R)]

    def adjoint_terms(w, first):
        wrow[...] = w

        def period(p, _):
            if first:
                pltpu.make_async_copy(blocks.at[p], bv.at[p], bsem.at[p]).wait()
            for r in range(NB):
                wv = wrow[pl.ds(r * NP + p, 1), :]
                col = jnp.sum(
                    jnp.where(eye, jnp.broadcast_to(wv, (B, B)), 0.0), axis=1, keepdims=True
                )
                wb = jnp.broadcast_to(col, (B, B))
                for k in range(K):
                    terms[p, r * K + k : r * K + k + 1, :] = jnp.sum(
                        bv[p, r, k] * wb, axis=0, keepdims=True
                    )
            return 0

        lax.fori_loop(0, NP, period, 0, unroll=8)
        t = terms[...].reshape(NP * TP, B)
        hi = t.astype(BF)
        rest = t - hi.astype(F32)
        mid = rest.astype(BF)
        low = (rest - mid.astype(F32)).astype(BF)
        oh = onehot[...]
        part = (
            jnp.dot(oh, low, preferred_element_type=F32)
            + jnp.dot(oh, mid, preferred_element_type=F32)
        ) + jnp.dot(oh, hi, preferred_element_type=F32)
        ps[...] = part[: D * R]
        for d in range(D):
            pb[d] = part[D * R + d * NB : D * R + (d + 1) * NB]

    def adjoint_sends(i):
        src = lambda d: my_rows(ps.at, d)
        main = lambda o: main_copy(src, my_rows(ra.at[i].at, me_d), rcv_a.at[i], o)
        edge = lambda o: edge_copy(lambda d: pb.at[d], rb.at[i, me_d], rcv_a.at[i], prev_s, o)
        loop(1, D, lambda o: main(o).start())
        loop(0, D, lambda o: edge(o).start())
        return main, edge

    def adjoint_result(i, main, edge):
        ra[i, pl.ds(pl.multiple_of(me_d * R, R), R), :] = ps[
            pl.ds(pl.multiple_of(me_d * R, R), R), :
        ]
        loop(1, D, lambda o: main(o).wait())
        loop(0, D, lambda o: edge(o).wait())
        total = ra[i, 0:R, :]
        rim = rb[i, 0]
        for d in range(1, D):
            total = total + ra[i, d * R : (d + 1) * R, :]
            rim = rim + rb[i, d]
        for c in range(NB):
            total = total + jnp.where(
                riota == c * NP + NP - 1, jnp.broadcast_to(rim[c : c + 1], (R, B)), 0.0
            )
        return total

    def forward(i, xbar):
        xs[...] = xbar
        for c in range(NB):
            xb[c : c + 1, :] = xbar[c * NP + NP - 1 : c * NP + NP]
        main = lambda o: main_copy(lambda d: xs, my_rows(g.at[i].at, me_d), rcv_f.at[i], o)
        edge = lambda o: edge_copy(lambda d: xb, gb.at[i, me_d], rcv_f.at[i], next_s, o)
        loop(1, D, lambda o: main(o).start())
        loop(0, D, lambda o: edge(o).start())
        g[i, pl.ds(pl.multiple_of(me_d * R, R), R), :] = xbar
        loop(1, D, lambda o: main(o).wait())
        loop(0, D, lambda o: edge(o).wait())

        def period(p, y):
            for r in range(NB):
                acc = None
                for k in range(K):
                    q = bp[k, r, p] - me_s * NP
                    col = ci[k, r, p]
                    d = lax.div(col, NB)
                    c = col - d * NB
                    row = d * R + c * NP + jnp.maximum(q, 0)
                    xv = g[i, pl.ds(row, 1), :]
                    if k > 0:
                        xv = jnp.where(q < 0, gb[i, d, pl.ds(c, 1), :], xv)
                    term = bv[p, r, k] * jnp.broadcast_to(xv, (B, B))
                    acc = term if acc is None else acc + term
                y = jnp.where(jj == r * NP + p, jnp.sum(acc, axis=1, keepdims=True), y)
            return y

        y = lax.fori_loop(0, NP, period, jnp.zeros((B, B), F32), unroll=8)
        return y.T[:R]

    w0 = jnp.full((1, B), pw[0], F32)
    tau0 = step_scale / w0
    sigma0 = step_scale * w0

    adjoint_terms(own_rows(y0r), True)
    for c in staged[3:]:
        c.wait()
    pl.semaphore_wait(barrier, N - 1)
    main, edge = adjoint_sends(0)
    at = adjoint_result(0, main, edge)
    x0 = own_rows(x0r)
    x1 = jnp.maximum(0.0, x0 - tau0 * (own_rows(cost) - at))
    x1s[...] = x1
    ax = forward(0, 2.0 * x1 - x0)
    y0 = own_rows(y0r)
    y1 = y0 + sigma0 * (own_rows(demand) - ax)
    y1s[...] = y1
    ds[0:1, :] = jnp.sum((x1s[...] - own_rows(x0r)) ** 2, axis=0, keepdims=True)
    ds[1:2, :] = jnp.sum((y1 - y0) ** 2, axis=0, keepdims=True)

    def dom_sum(o):
        d = lax.rem(me_d + o, D)
        return pltpu.make_async_remote_copy(
            src_ref=ds, dst_ref=dg.at[me_d], send_sem=snd_d.at[o], recv_sem=rcv_d.at[o],
            device_id={"section": me_s, "dom": d}, device_id_type=MESH,
        )

    def section_sum(o):
        s = lax.rem(me_s + o, S)
        return pltpu.make_async_remote_copy(
            src_ref=es, dst_ref=eg.at[me_s], send_sem=snd_e.at[o], recv_sem=rcv_e.at[o],
            device_id={"section": s, "dom": me_d}, device_id_type=MESH,
        )

    loop(1, D, lambda o: dom_sum(o).start())
    dg[me_d] = ds[...]
    adjoint_terms(y1, False)
    main, edge = adjoint_sends(1)
    loop(1, D, lambda o: dom_sum(o).wait())
    moved = dg[0]
    for d in range(1, D):
        moved = moved + dg[d]
    es[...] = moved
    loop(1, S, lambda o: section_sum(o).start())
    eg[me_s] = moved
    loop(1, S, lambda o: section_sum(o).wait())
    moved = eg[0]
    for s in range(1, S):
        moved = moved + eg[s]
    moved = jnp.sum(moved, axis=1, keepdims=True)
    dx = jnp.broadcast_to(moved[0:1], (1, B))
    dy = jnp.broadcast_to(moved[1:2], (1, B))
    omega = jnp.sqrt(w0 * jnp.sqrt((dy + epsilon) / (dx + epsilon)))
    tau1 = step_scale / omega
    sigma1 = step_scale * omega
    at = adjoint_result(1, main, edge)
    x1 = x1s[...]
    x2 = jnp.maximum(0.0, x1 - tau1 * (own_rows(cost) - at))
    for c in range(NB):
        xo[:, c * B : (c + 1) * B] = x2[c * NP : (c + 1) * NP]
    ax = forward(1, 2.0 * x2 - x1)
    y2 = y1s[...] + sigma1 * (own_rows(demand) - ax)
    for c in range(NB):
        yo[:, c * B : (c + 1) * B] = y2[c * NP : (c + 1) * NP]


def on_device(S, D, blocks, ci, bp, cost, demand, x0, y0, pw):
    NP, NB, K, B, _ = blocks.shape
    R = NB * NP
    TP = -(-NB * K // 8) * 8
    M = D * R + D * NB
    vmem = pl.BlockSpec(memory_space=pltpu.VMEM)
    smem = pl.BlockSpec(memory_space=pltpu.SMEM)
    hbm = pl.BlockSpec(memory_space=pl.ANY)
    V = lambda *s: pltpu.VMEM(s, F32)
    sem = lambda *s: pltpu.SemaphoreType.DMA(s)
    return pl.pallas_call(
        functools.partial(kernel_body, S, D, NP, NB, K, B),
        out_shape=(
            jax.ShapeDtypeStruct(x0.shape, F32),
            jax.ShapeDtypeStruct(y0.shape, F32),
        ),
        in_specs=[hbm, hbm, hbm, hbm, hbm, hbm, hbm, smem],
        out_specs=(vmem, vmem),
        scratch_shapes=[
            pltpu.SMEM((K, NB, NP), jnp.int32),
            pltpu.SMEM((K, NB, NP), jnp.int32),
            V(*cost.shape),
            V(*cost.shape),
            V(*cost.shape),
            V(*cost.shape),
            sem(6),
            V(NP, NB, K, B, B),
            pltpu.VMEM((M, NP * TP), BF),
            V(NP, TP, B),
            V(R, B),
            V(D * R, B),
            V(D, NB, B),
            V(2, D * R, B),
            V(2, D, NB, B),
            V(R, B),
            V(NB, B),
            V(2, D * R, B),
            V(2, D, NB, B),
            V(R, B),
            V(R, B),
            V(2, B),
            V(D, 2, B),
            V(2, B),
            V(S, 2, B),
            sem(NP),
            sem(2, D),
            sem(2, 2, D),
            sem(2, 2, D),
            sem(D),
            sem(D),
            sem(S),
            sem(S),
        ],
        compiler_params=pltpu.CompilerParams(
            collective_id=0, has_side_effects=True, vmem_limit_bytes=48 * 1024 * 1024
        ),
    )(*[
        pltpu.with_memory_space_constraint(v, pltpu.HBM)
        for v in (blocks, ci.transpose(2, 1, 0), bp.transpose(2, 1, 0), cost, demand, x0, y0)
    ], pw)


def solution(mesh):
    return jax.shard_map(
        functools.partial(on_device, mesh.shape["section"], mesh.shape["dom"]),
        mesh=mesh,
        in_specs=(
            P("section", "dom", None, None, None),
            P("section", "dom", None),
            P("section", "dom", None),
            P("section", "dom"),
            P("section", "dom"),
            P("section", "dom"),
            P("section", "dom"),
            P(),
        ),
        out_specs=(P("section", "dom"), P("section", "dom")),
        check_vma=False,
    )
```

```python
import functools

import jax
import jax.numpy as jnp
from jax import lax
from jax.experimental import pallas as pl
from jax.experimental.pallas import tpu as pltpu
from jax.sharding import PartitionSpec as P

step_scale = 0.4
epsilon = 1e-06
MESH = pl.DeviceIdType.MESH
BF = jnp.bfloat16
F32 = jnp.float32


def kernel_body(
    S, D, NP, NB, K, B,
    blocks, ci_in, bp_in, cost_in, demand_in, x0_in, y0_in, pw,
    xo, yo,
    ci, bp, cost, demand, x0r, y0r, isem,
    bv, onehot, terms, wrow, ps, pb, ra, rb, xs, xb, g, gb, x1s, y1s, ds, dg, es, eg,
    bsem, snd, rcv_a, rcv_f, snd_d, rcv_d, snd_e, rcv_e,
):
    R = NB * NP
    TP = terms.shape[1]
    N = S * D
    me_s = lax.axis_index("section")
    me_d = lax.axis_index("dom")
    me = me_s * D + me_d
    prev_s = lax.rem(me_s + S - 1, S)
    next_s = lax.rem(me_s + 1, S)

    barrier = pltpu.get_barrier_semaphore()

    def greet(t, _):
        other = lax.rem(me + t, N)
        pl.semaphore_signal(
            barrier,
            inc=1,
            device_id={"section": lax.div(other, D), "dom": lax.rem(other, D)},
            device_id_type=MESH,
        )
        return 0

    staged = [
        pltpu.make_async_copy(a, b, isem.at[i])
        for i, (a, b) in enumerate(
            ((y0_in, y0r), (ci_in, ci), (bp_in, bp), (cost_in, cost), (x0_in, x0r), (demand_in, demand))
        )
    ]
    for c in staged[:3]:
        c.start()
    for p in range(NP):
        pltpu.make_async_copy(blocks.at[p], bv.at[p], bsem.at[p]).start()
    for c in staged[3:]:
        c.start()
    rb[...] = jnp.zeros_like(rb)
    gb[...] = jnp.zeros_like(gb)
    lax.fori_loop(1, N, greet, 0)

    for c in staged[:3]:
        c.wait()

    def own_rows(ref):
        return jnp.concatenate([ref[:, c * B : (c + 1) * B] for c in range(NB)], axis=0)

    lane = lax.broadcasted_iota(jnp.int32, (1, NP * TP), 1)
    target = jnp.full((1, NP * TP), -1, jnp.int32)
    for p in range(NP):
        for r in range(NB):
            for k in range(K):
                q = bp[k, r, p] - me_s * NP
                col = ci[k, r, p]
                d = lax.div(col, NB)
                c = col - d * NB
                row = jnp.where(q < 0, D * R + col, d * R + c * NP + q)
                target = jnp.where(lane == p * TP + r * K + k, row, target)
    M = onehot.shape[0]
    rows_m = lax.broadcasted_iota(jnp.int32, (M, NP * TP), 0)
    onehot[...] = jnp.where(rows_m == target, 1.0, 0.0).astype(BF)
    terms[...] = jnp.zeros_like(terms)

    ii = lax.broadcasted_iota(jnp.int32, (B, B), 0)
    jj = lax.broadcasted_iota(jnp.int32, (B, B), 1)
    eye = ii == jj
    riota = lax.broadcasted_iota(jnp.int32, (R, B), 0)

    def main_copy(src, dst, recv, o):
        d = lax.rem(me_d + o, D)
        return pltpu.make_async_remote_copy(
            src_ref=src(d), dst_ref=dst, send_sem=snd.at[0, o], recv_sem=recv.at[0, o],
            device_id={"section": me_s, "dom": d}, device_id_type=MESH,
        )

    def edge_copy(src, dst, recv, sec, o):
        d = lax.rem(me_d + o, D)
        return pltpu.make_async_remote_copy(
            src_ref=src(d), dst_ref=dst, send_sem=snd.at[1, o], recv_sem=recv.at[1, o],
            device_id={"section": sec, "dom": d}, device_id_type=MESH,
        )

    def loop(lo, hi, f):
        def step(o, _):
            f(o)
            return 0

        lax.fori_loop(lo, hi, step, 0, unroll=True)

    def my_rows(ref_at, d):
        return ref_at[pl.ds(pl.multiple_of(d * R, R), R)]

    def adjoint_terms(w, first):
        wrow[...] = w

        def period(p, _):
            if first:
                pltpu.make_async_copy(blocks.at[p], bv.at[p], bsem.at[p]).wait()
            for r in range(NB):
                wv = wrow[pl.ds(r * NP + p, 1), :]
                col = jnp.sum(
                    jnp.where(eye, jnp.broadcast_to(wv, (B, B)), 0.0), axis=1, keepdims=True
                )
                wb = jnp.broadcast_to(col, (B, B))
                for k in range(K):
                    terms[p, r * K + k : r * K + k + 1, :] = jnp.sum(
                        bv[p, r, k] * wb, axis=0, keepdims=True
                    )
            return 0

        lax.fori_loop(0, NP, period, 0, unroll=8)
        t = terms[...].reshape(NP * TP, B)
        hi = t.astype(BF)
        rest = t - hi.astype(F32)
        mid = rest.astype(BF)
        low = (rest - mid.astype(F32)).astype(BF)
        oh = onehot[...]
        part = (
            jnp.dot(oh, low, preferred_element_type=F32)
            + jnp.dot(oh, mid, preferred_element_type=F32)
        ) + jnp.dot(oh, hi, preferred_element_type=F32)
        ps[...] = part[: D * R]
        for d in range(D):
            pb[d] = part[D * R + d * NB : D * R + (d + 1) * NB]

    def adjoint_sends(i):
        src = lambda d: my_rows(ps.at, d)
        main = lambda o: main_copy(src, my_rows(ra.at[i].at, me_d), rcv_a.at[i], o)
        edge = lambda o: edge_copy(lambda d: pb.at[d], rb.at[i, me_d], rcv_a.at[i], prev_s, o)
        loop(1, D, lambda o: main(o).start())
        pl.when(me_s > 0)(lambda: loop(0, D, lambda o: edge(o).start()))
        return main, edge

    def adjoint_result(i, main, edge):
        ra[i, pl.ds(pl.multiple_of(me_d * R, R), R), :] = ps[
            pl.ds(pl.multiple_of(me_d * R, R), R), :
        ]
        loop(1, D, lambda o: main(o).wait())
        pl.when(me_s > 0)(lambda: loop(0, D, lambda o: edge(o).wait_send()))
        pl.when(me_s < S - 1)(lambda: loop(0, D, lambda o: edge(o).wait_recv()))
        total = ra[i, 0:R, :]
        rim = rb[i, 0]
        for d in range(1, D):
            total = total + ra[i, d * R : (d + 1) * R, :]
            rim = rim + rb[i, d]
        for c in range(NB):
            total = total + jnp.where(
                riota == c * NP + NP - 1, jnp.broadcast_to(rim[c : c + 1], (R, B)), 0.0
            )
        return total

    def forward(i, xbar):
        xs[...] = xbar
        for c in range(NB):
            xb[c : c + 1, :] = xbar[c * NP + NP - 1 : c * NP + NP]
        main = lambda o: main_copy(lambda d: xs, my_rows(g.at[i].at, me_d), rcv_f.at[i], o)
        edge = lambda o: edge_copy(lambda d: xb, gb.at[i, me_d], rcv_f.at[i], next_s, o)
        loop(1, D, lambda o: main(o).start())
        pl.when(me_s < S - 1)(lambda: loop(0, D, lambda o: edge(o).start()))
        g[i, pl.ds(pl.multiple_of(me_d * R, R), R), :] = xbar
        loop(1, D, lambda o: main(o).wait())
        pl.when(me_s < S - 1)(lambda: loop(0, D, lambda o: edge(o).wait_send()))
        pl.when(me_s > 0)(lambda: loop(0, D, lambda o: edge(o).wait_recv()))

        def period(p, y):
            for r in range(NB):
                acc = None
                for k in range(K):
                    q = bp[k, r, p] - me_s * NP
                    col = ci[k, r, p]
                    d = lax.div(col, NB)
                    c = col - d * NB
                    row = d * R + c * NP + jnp.maximum(q, 0)
                    xv = g[i, pl.ds(row, 1), :]
                    if k > 0:
                        xv = jnp.where(q < 0, gb[i, d, pl.ds(c, 1), :], xv)
                    term = bv[p, r, k] * jnp.broadcast_to(xv, (B, B))
                    acc = term if acc is None else acc + term
                y = jnp.where(jj == r * NP + p, jnp.sum(acc, axis=1, keepdims=True), y)
            return y

        y = lax.fori_loop(0, NP, period, jnp.zeros((B, B), F32), unroll=8)
        return y.T[:R]

    w0 = jnp.full((1, B), pw[0], F32)
    tau0 = step_scale / w0
    sigma0 = step_scale * w0

    adjoint_terms(own_rows(y0r), True)
    for c in staged[3:]:
        c.wait()
    pl.semaphore_wait(barrier, N - 1)
    main, edge = adjoint_sends(0)
    at = adjoint_result(0, main, edge)
    x0 = own_rows(x0r)
    x1 = jnp.maximum(0.0, x0 - tau0 * (own_rows(cost) - at))
    x1s[...] = x1
    ax = forward(0, 2.0 * x1 - x0)
    y0 = own_rows(y0r)
    y1 = y0 + sigma0 * (own_rows(demand) - ax)
    y1s[...] = y1
    ds[0:1, :] = jnp.sum((x1s[...] - own_rows(x0r)) ** 2, axis=0, keepdims=True)
    ds[1:2, :] = jnp.sum((y1 - y0) ** 2, axis=0, keepdims=True)

    def dom_sum(o):
        d = lax.rem(me_d + o, D)
        return pltpu.make_async_remote_copy(
            src_ref=ds, dst_ref=dg.at[me_d], send_sem=snd_d.at[o], recv_sem=rcv_d.at[o],
            device_id={"section": me_s, "dom": d}, device_id_type=MESH,
        )

    def section_sum(o):
        s = lax.rem(me_s + o, S)
        return pltpu.make_async_remote_copy(
            src_ref=es, dst_ref=eg.at[me_s], send_sem=snd_e.at[o], recv_sem=rcv_e.at[o],
            device_id={"section": s, "dom": me_d}, device_id_type=MESH,
        )

    loop(1, D, lambda o: dom_sum(o).start())
    dg[me_d] = ds[...]
    adjoint_terms(y1, False)
    main, edge = adjoint_sends(1)
    loop(1, D, lambda o: dom_sum(o).wait())
    moved = dg[0]
    for d in range(1, D):
        moved = moved + dg[d]
    es[...] = moved
    loop(1, S, lambda o: section_sum(o).start())
    eg[me_s] = moved
    loop(1, S, lambda o: section_sum(o).wait())
    moved = eg[0]
    for s in range(1, S):
        moved = moved + eg[s]
    moved = jnp.sum(moved, axis=1, keepdims=True)
    dx = jnp.broadcast_to(moved[0:1], (1, B))
    dy = jnp.broadcast_to(moved[1:2], (1, B))
    omega = jnp.sqrt(w0 * jnp.sqrt((dy + epsilon) / (dx + epsilon)))
    tau1 = step_scale / omega
    sigma1 = step_scale * omega
    at = adjoint_result(1, main, edge)
    x1 = x1s[...]
    x2 = jnp.maximum(0.0, x1 - tau1 * (own_rows(cost) - at))
    for c in range(NB):
        xo[:, c * B : (c + 1) * B] = x2[c * NP : (c + 1) * NP]
    ax = forward(1, 2.0 * x2 - x1)
    y2 = y1s[...] + sigma1 * (own_rows(demand) - ax)
    for c in range(NB):
        yo[:, c * B : (c + 1) * B] = y2[c * NP : (c + 1) * NP]


def on_device(S, D, blocks, ci, bp, cost, demand, x0, y0, pw):
    NP, NB, K, B, _ = blocks.shape
    R = NB * NP
    TP = -(-NB * K // 8) * 8
    M = D * R + D * NB
    vmem = pl.BlockSpec(memory_space=pltpu.VMEM)
    smem = pl.BlockSpec(memory_space=pltpu.SMEM)
    hbm = pl.BlockSpec(memory_space=pl.ANY)
    V = lambda *s: pltpu.VMEM(s, F32)
    sem = lambda *s: pltpu.SemaphoreType.DMA(s)
    return pl.pallas_call(
        functools.partial(kernel_body, S, D, NP, NB, K, B),
        out_shape=(
            jax.ShapeDtypeStruct(x0.shape, F32),
            jax.ShapeDtypeStruct(y0.shape, F32),
        ),
        in_specs=[hbm, hbm, hbm, hbm, hbm, hbm, hbm, smem],
        out_specs=(vmem, vmem),
        scratch_shapes=[
            pltpu.SMEM((K, NB, NP), jnp.int32),
            pltpu.SMEM((K, NB, NP), jnp.int32),
            V(*cost.shape),
            V(*cost.shape),
            V(*cost.shape),
            V(*cost.shape),
            sem(6),
            V(NP, NB, K, B, B),
            pltpu.VMEM((M, NP * TP), BF),
            V(NP, TP, B),
            V(R, B),
            V(D * R, B),
            V(D, NB, B),
            V(2, D * R, B),
            V(2, D, NB, B),
            V(R, B),
            V(NB, B),
            V(2, D * R, B),
            V(2, D, NB, B),
            V(R, B),
            V(R, B),
            V(2, B),
            V(D, 2, B),
            V(2, B),
            V(S, 2, B),
            sem(NP),
            sem(2, D),
            sem(2, 2, D),
            sem(2, 2, D),
            sem(D),
            sem(D),
            sem(S),
            sem(S),
        ],
        compiler_params=pltpu.CompilerParams(
            collective_id=0, has_side_effects=True, vmem_limit_bytes=48 * 1024 * 1024
        ),
    )(*[
        pltpu.with_memory_space_constraint(v, pltpu.HBM)
        for v in (blocks, ci.transpose(2, 1, 0), bp.transpose(2, 1, 0), cost, demand, x0, y0)
    ], pw)


def solution(mesh):
    return jax.shard_map(
        functools.partial(on_device, mesh.shape["section"], mesh.shape["dom"]),
        mesh=mesh,
        in_specs=(
            P("section", "dom", None, None, None),
            P("section", "dom", None),
            P("section", "dom", None),
            P("section", "dom"),
            P("section", "dom"),
            P("section", "dom"),
            P("section", "dom"),
            P(),
        ),
        out_specs=(P("section", "dom"), P("section", "dom")),
        check_vma=False,
    )
```
